256 devices in a mesh: ga: 64 (over z, y, x_hi), gp: 4 (over x_lo, core).
Axes of the slice: x: 4 (x_hi: 2, x_lo: 2; x = x_hi * 2 + x_lo), y: 4, z: 8, core: 2. Of those that a mesh axis runs over, the one named last changes fastest.
Arguments:
- screened: bfloat16 [16384, 65536], P('ga', 'gp'), may hold values from -0.0234375 to 0.0234375
- valence: bfloat16 [64, 32, 65536], P('ga', None, 'gp'), may hold values from -6 to 6
- conduction: bfloat16 [1024, 16384], P(None, 'ga'), may hold values from -0.125 to 0.125
- owner: int32 [6], replicated, may hold values from 0 to 63
Outputs:
- kernel: float32 [1024, 192], P('ga', 'gp')
The draws below stay inside these ranges and needn't reach their ends.
Inputs may be any that keep to these rules, and one draw needn't show every extreme that they name: owner[b] is the slot of valence, along its first dimension, that holds batch b.
All inputs are finite; a program needn't handle non-finite values.
Results may differ from the reference program's by a relative error of at most 0.0003.
Values may be sent and summed in bfloat16 or wider, within the bound.
No kernel may reach another device: no remote copies, remote signals or barrier semaphores. Data moves between devices by JAX's collectives and lax.ppermute only.
A program may use at most 64 MiB of HBM per device.

```python
import jax
import jax.numpy as jnp
from jax import lax

NG = 65536
NV = 32
NC = 1024
NB = 6
GROWS = 16384
SLOTS = 64
N_GA = 64


def touch_ends(drawn, rng, smallest, largest):
    longest = drawn.shape.index(max(drawn.shape))
    spots = []
    for shift in (0, 1):
        where = [jax.random.randint(jax.random.fold_in(rng, axis), (), 0, length) for axis, length in enumerate(drawn.shape)]
        where[longest] = (where[longest] + shift) % drawn.shape[longest]
        spots.append(tuple(where))
    return drawn.at[spots[0]].set(smallest).at[spots[1]].set(largest)


def strengthened(drawn, rng, source, target, blocks, factor):
    def block_of(position):
        return (jnp.arange(drawn.shape[position]) // (drawn.shape[position] // blocks)).reshape((-1,) + (1,) * (drawn.ndim - 1 - position))

    one_side = jax.random.permutation(rng, blocks)[block_of(target)]
    second = (block_of(target) + blocks // 2) % blocks
    return jnp.where((block_of(source) == one_side) | (block_of(source) == second), factor * drawn, drawn)


def steps_of(own_key, dims, pieces, smallest, high):
    factor_of = 1.0
    for position, shards_of in pieces:
        draws = jax.random.uniform(jax.random.fold_in(jax.random.fold_in(own_key, 6), position), (shards_of,), jnp.float32, smallest / len(pieces), high / len(pieces))
        factor_of = factor_of * jnp.repeat(jnp.exp(draws), dims[position] // shards_of).reshape((-1,) + (1,) * (len(dims) - 1 - position))
    return factor_of


def gaussian(key, dims, width, most, pieces=(), dtype=jnp.bfloat16):
    entries = width * jax.random.normal(key, dims, jnp.float32)
    if pieces:
        entries = entries * steps_of(key, dims, pieces, -0.22, 0.18)
    return jnp.clip(entries, -most, most).astype(dtype)


def gaussian_with(own_key, dims, deviation, reach, cuts, heavy, kind=jnp.bfloat16):
    drawn = deviation * jax.random.normal(own_key, dims, jnp.float32)
    if cuts:
        drawn = drawn * steps_of(own_key, dims, cuts, -0.22, 0.18)
    return jnp.clip(strengthened(drawn, jax.random.fold_in(own_key, 3), *heavy), -reach, reach).astype(kind)


def setup_inputs(seed: int = 0) -> dict:
    key_list = jax.random.split(jax.random.key(seed), 5)
    screened = gaussian(key_list[0], (GROWS, NG), NG ** -0.5, 0.0234375, ((0, 64), (1, 4)))
    valence = gaussian(key_list[1], (SLOTS, NV, NG), 1.0, 6.0, ((0, 64), (2, 4)))
    conduction = gaussian_with(key_list[2], (NC, GROWS), GROWS ** -0.5, 0.125, ((1, 64),), (1, 0, 64, 4.0))
    owner = touch_ends(jax.random.randint(key_list[3], (NB,), 0, N_GA), jax.random.fold_in(key_list[3], 1), 0, N_GA - 1).astype(jnp.int32)
    return dict(screened=screened, valence=valence, conduction=conduction, owner=owner)


def reference(screened, valence, conduction, owner):
    chosen = valence[owner.astype(jnp.int32)]
    stacked = chosen.reshape(chosen.shape[0] * chosen.shape[1], chosen.shape[2])
    pair = lax.dot_general(screened, stacked, (((1,), (1,)), ((), ())), preferred_element_type=jnp.float32)
    kernel = jnp.dot(conduction.astype(jnp.float32), pair, precision=lax.Precision.HIGHEST)
    return kernel
```

```python
import functools

import jax
import jax.numpy as jnp
from jax import lax
from jax.experimental import pallas as pl
from jax.experimental.pallas import tpu as pltpu
from jax.sharding import Mesh, PartitionSpec as P

NZ, NY, NX, NGP = 8, 4, 2, 4
K = 256
F32, BF16 = jnp.float32, jnp.bfloat16


def shift(x, axis, n, d):
    return lax.ppermute(x, axis, [(i, (i + d) % n) for i in range(n)])


def accumulate(offs_ref, w_ref, blocks, wbuf, sems, acc):
    flat = [(ref, i) for ref in blocks for i in range(ref.shape[0])]
    copies = []
    for n in range(len(flat)):
        column = pl.multiple_of(offs_ref[n], K)
        copy = pltpu.make_async_copy(w_ref.at[:, pl.ds(column, K)], wbuf.at[n], sems.at[n])
        copy.start()
        copies.append(copy)
    for n, (ref, i) in enumerate(flat):
        copies[n].wait()
        acc = acc + lax.dot_general(ref[i], wbuf[n], (((1,), (1,)), ((), ())), preferred_element_type=F32)
    return acc


def pair_kernel(n_blocks, first, offs_ref, w_ref, *refs):
    blocks, rest = refs[:n_blocks], refs[n_blocks:]
    if first:
        out_ref, wbuf, sems = rest
        acc = jnp.zeros(out_ref.shape, F32)
    else:
        acc_ref, out_ref, wbuf, sems = rest
        acc = acc_ref[...]
    out_ref[...] = accumulate(offs_ref, w_ref, blocks, wbuf, sems, acc)


def pair_call(w, blocks, offs, acc=None):
    n = sum(b.shape[0] for b in blocks)
    rows, g = blocks[0].shape[1], w.shape[0]
    vm = pl.BlockSpec(memory_space=pltpu.VMEM)
    args = [jnp.stack(offs).astype(jnp.int32), w, *blocks] + ([] if acc is None else [acc])
    return pl.pallas_call(
        functools.partial(pair_kernel, len(blocks), acc is None),
        out_shape=jax.ShapeDtypeStruct((rows, g), F32),
        in_specs=[pl.BlockSpec(memory_space=pltpu.SMEM), pl.BlockSpec(memory_space=pl.ANY)] + [vm] * (len(args) - 2),
        out_specs=vm,
        scratch_shapes=[pltpu.VMEM((n, g, K), BF16), pltpu.SemaphoreType.DMA((n,))],
        compiler_params=pltpu.CompilerParams(vmem_limit_bytes=32 << 20),
        cost_estimate=pl.CostEstimate(flops=2 * n * rows * g * K, bytes_accessed=n * (rows + g) * K * 2, transcendentals=0),
    )(*args)


def term_kernel(a_ref, b_ref, c_ref, d_ref, cond_ref, out_ref):
    total = (a_ref[...] + b_ref[...]) + (c_ref[...] + d_ref[...])
    rows = total.shape[0]
    hi = total.astype(BF16)
    rest = total - hi.astype(F32)
    mid = rest.astype(BF16)
    low = (rest - mid.astype(F32)).astype(BF16)
    stacked = jnp.concatenate([hi, mid, low], axis=0)
    prod = lax.dot_general(stacked, cond_ref[...], (((1,), (1,)), ((), ())), preferred_element_type=F32)
    term = prod[:rows] + (prod[rows:2 * rows] + prod[2 * rows:])
    width = out_ref.shape[2]
    for z in range(out_ref.shape[0]):
        out_ref[z] = term[:, z * width:(z + 1) * width]


def term_call(parts, cond):
    rows, nc = parts[0].shape[0], cond.shape[0]
    vm = pl.BlockSpec(memory_space=pltpu.VMEM)
    return pl.pallas_call(
        term_kernel,
        out_shape=jax.ShapeDtypeStruct((NZ, rows, nc // NZ), F32),
        in_specs=[vm] * 5,
        out_specs=vm,
        cost_estimate=pl.CostEstimate(flops=6 * rows * nc * cond.shape[1], bytes_accessed=nc * cond.shape[1] * 2, transcendentals=0),
    )(*parts, cond)


def body(screened, valence, conduction, owner):
    nb = owner.shape[0]
    _, nv, ncol = valence.shape
    half = ncol // 2
    z, y, xh = lax.axis_index("z"), lax.axis_index("y"), lax.axis_index("xh")
    gp = lax.axis_index("xl") * 2 + lax.axis_index("c")
    lane = half // (NZ * NY * NX)

    own = valence[0]
    part_a = own[:, :half].reshape(nv, NZ, NY, NX, lane).transpose(1, 2, 3, 0, 4)
    part_b = own[:, half:].reshape(nv, NY, NZ, NX, lane).transpose(2, 1, 3, 0, 4)
    pieces = jnp.concatenate([part_a, part_b], axis=-1).reshape(NZ * NY * NX, nv, 2 * lane)
    recv = lax.all_to_all(pieces, ("z", "y", "xh"), 0, 0, tiled=True)
    mine = jnp.concatenate([lax.dynamic_index_in_dim(recv, owner[b], 0, keepdims=False) for b in range(nb)], axis=0)

    other = shift(mine, "xh", NX, 1)
    lo, hi = jnp.where(xh == 0, mine, other), jnp.where(xh == 0, other, mine)
    a = jnp.concatenate([lo[:, :lane], hi[:, :lane]], axis=1)
    b = jnp.concatenate([lo[:, lane:], hi[:, lane:]], axis=1)

    def col_a(dz, dy):
        return (((z + dz) % NZ) * NY + (y + dy) % NY) * K

    def col_b(dz, dy):
        return half + (((y + dy) % NY) * NZ + (z + dz) % NZ) * K

    ya = [a, shift(a, "y", NY, 1), shift(a, "y", NY, -1), shift(a, "y", NY, 2)]
    dys = [0, -1, 1, -2]
    zr = zl = b
    zb, dzs = [b], [0]
    hb = b.shape[0] // 2
    for s in (1, 2, 3):
        zr, zl = shift(zr, "z", NZ, 1), shift(zl, "z", NZ, -1)
        zb += [zr, zl]
        dzs += [-s, s]
    zb.append(jnp.concatenate([shift(zr[:hb], "z", NZ, 1), shift(zl[hb:], "z", NZ, -1)], axis=0))
    dzs.append(4)
    sa = jnp.stack(ya)
    sb = jnp.stack(zb)

    blocks1, offs1 = [sa, sb], [col_a(0, d) for d in dys] + [col_b(d, 0) for d in dzs]
    ar = al = sa
    for s in (1, 2):
        ar, al = shift(ar, "z", NZ, 1), shift(al, "z", NZ, -1)
        blocks1 += [ar, al]
        offs1 += [col_a(-s, d) for d in dys] + [col_a(s, d) for d in dys]
    br, bl = shift(sb, "y", NY, 1), shift(sb, "y", NY, -1)
    ar, al = shift(ar, "z", NZ, 1), shift(al, "z", NZ, -1)
    blocks2 = [ar, al, br, bl]
    offs2 = [col_a(-3, d) for d in dys] + [col_a(3, d) for d in dys] + [col_b(d, -1) for d in dzs] + [col_b(d, 1) for d in dzs]
    a4r, a4l = shift(ar[:2], "z", NZ, 1), shift(al[2:], "z", NZ, -1)
    b2r, b2l = shift(br[:4], "y", NY, 1), shift(bl[4:], "y", NY, -1)
    blocks3 = [a4r, a4l, b2r, b2l]
    offs3 = [col_a(4, d) for d in dys] + [col_b(d, 2) for d in dzs]

    acc = pair_call(screened, blocks1, offs1)
    acc = pair_call(screened, blocks2, offs2, acc)
    acc = pair_call(screened, blocks3, offs3, acc)

    wide = acc.reshape(NGP, acc.shape[0] // NGP, acc.shape[1])
    parts = [lax.dynamic_index_in_dim(wide, gp, 0, keepdims=False)]
    for k in (1, 2, 3):
        out = lax.dynamic_index_in_dim(wide, gp ^ k, 0, keepdims=False)
        parts.append(lax.ppermute(out, ("xl", "c"), [(i, i ^ k) for i in range(NGP)]))
    term = term_call(parts, conduction)

    zsum = jnp.sum(lax.all_to_all(term, "z", 0, 0, tiled=True), axis=0)
    rows = zsum.T.reshape(NY * NX, zsum.shape[1] // (NY * NX), zsum.shape[0])
    return jnp.sum(lax.all_to_all(rows, ("y", "xh"), 0, 0, tiled=True), axis=0)


def solution(mesh):
    fine = Mesh(mesh.devices.reshape(NZ, NY, NX, 2, 2), ("z", "y", "xh", "xl", "c"))
    ga, gp = ("z", "y", "xh"), ("xl", "c")
    placed = (P(ga, gp), P(ga, None, gp), P(None, ga), P())
    return jax.shard_map(body, mesh=fine, in_specs=placed, out_specs=P(ga, gp), check_vma=False)
```

```python
import functools

import jax
import jax.numpy as jnp
from jax import lax
from jax.experimental import pallas as pl
from jax.experimental.pallas import tpu as pltpu
from jax.sharding import Mesh, PartitionSpec as P

NZ, NY, NX, NGP = 8, 4, 2, 4
K = 256
F32, BF16 = jnp.float32, jnp.bfloat16
VM = pl.BlockSpec(memory_space=pltpu.VMEM)
SM = pl.BlockSpec(memory_space=pltpu.SMEM)


def shift(x, axis, n, d):
    return lax.ppermute(x, axis, [(i, (i + d) % n) for i in range(n)])


def pack_kernel(lane, own_ref, out_ref):
    half = NZ * NY * NX * lane
    for z in range(NZ):
        for y in range(NY):
            for x in range(NX):
                p = (z * NY + y) * NX + x
                q = (y * NZ + z) * NX + x
                out_ref[p, :, :lane] = own_ref[0, :, p * lane:(p + 1) * lane]
                out_ref[p, :, lane:] = own_ref[0, :, half + q * lane:half + (q + 1) * lane]


def pack(valence):
    _, nv, ncol = valence.shape
    n = NZ * NY * NX
    lane = ncol // (2 * n)
    return pl.pallas_call(
        functools.partial(pack_kernel, lane),
        out_shape=jax.ShapeDtypeStruct((n, nv, 2 * lane), valence.dtype),
        in_specs=[VM],
        out_specs=VM,
        compiler_params=pltpu.CompilerParams(vmem_limit_bytes=8 << 20),
        cost_estimate=pl.CostEstimate(flops=0, bytes_accessed=4 * nv * ncol, transcendentals=0),
    )(valence)


def pair_kernel(places, first, last, me_ref, w_ref, *refs):
    blocks, rest = refs[:len(places)], refs[len(places):]
    z, y = me_ref[0], me_ref[1]
    half = w_ref.shape[1] // 2
    acc = None if first else rest[0][...]
    for ref, place in zip(blocks, places, strict=True):
        for i, (part, dz, dy) in enumerate(place):
            zz, yy = (z + dz) & (NZ - 1), (y + dy) & (NY - 1)
            column = (zz * NY + yy) * K if part == 0 else half + (yy * NZ + zz) * K
            w = w_ref[:, pl.ds(pl.multiple_of(column, K), K)]
            term = lax.dot_general(ref[i], w, (((1,), (1,)), ((), ())), preferred_element_type=F32)
            acc = term if acc is None else acc + term
    outs = rest[0 if first else 1:]
    if not last:
        outs[0][...] = acc
        return
    scratch = outs[NGP]
    scratch[...] = acc
    rows = outs[0].shape[0]
    for k in range(NGP):
        outs[k][...] = scratch[pl.ds(pl.multiple_of((me_ref[2] ^ k) * rows, 8), rows), :]


def pair_call(me, w, blocks, places, acc=None, last=False):
    n = sum(b.shape[0] for b in blocks)
    rows, g = blocks[0].shape[1], w.shape[0]
    args = [me, w, *blocks] + ([] if acc is None else [acc])
    whole = jax.ShapeDtypeStruct((rows, g), F32)
    share = jax.ShapeDtypeStruct((rows // NGP, g), F32)
    return pl.pallas_call(
        functools.partial(pair_kernel, places, acc is None, last),
        out_shape=[share] * NGP if last else whole,
        in_specs=[SM] + [VM] * (len(args) - 1),
        out_specs=[VM] * NGP if last else VM,
        scratch_shapes=[pltpu.VMEM((rows, g), F32)] if last else [],
        compiler_params=pltpu.CompilerParams(vmem_limit_bytes=16 << 20),
        cost_estimate=pl.CostEstimate(flops=2 * n * rows * g * K, bytes_accessed=n * (rows + g) * K * 2, transcendentals=0),
    )(*args)


def term_kernel(a_ref, b_ref, c_ref, d_ref, cond_ref, out_ref):
    total = (a_ref[...] + b_ref[...]) + (c_ref[...] + d_ref[...])
    rows = total.shape[0]
    hi = total.astype(BF16)
    rest = total - hi.astype(F32)
    mid = rest.astype(BF16)
    low = (rest - mid.astype(F32)).astype(BF16)
    stacked = jnp.concatenate([hi, mid, low], axis=0)
    prod = lax.dot_general(stacked, cond_ref[...], (((1,), (1,)), ((), ())), preferred_element_type=F32)
    term = prod[:rows] + (prod[rows:2 * rows] + prod[2 * rows:])
    width = out_ref.shape[2]
    for z in range(out_ref.shape[0]):
        out_ref[z] = term[:, z * width:(z + 1) * width]


def term_call(parts, cond):
    rows, nc = parts[0].shape[0], cond.shape[0]
    return pl.pallas_call(
        term_kernel,
        out_shape=jax.ShapeDtypeStruct((NZ, rows, nc // NZ), F32),
        in_specs=[VM] * 5,
        out_specs=VM,
        compiler_params=pltpu.CompilerParams(vmem_limit_bytes=8 << 20),
        cost_estimate=pl.CostEstimate(flops=6 * rows * nc * cond.shape[1], bytes_accessed=nc * cond.shape[1] * 2, transcendentals=0),
    )(*parts, cond)


def body(screened, valence, conduction, owner):
    nb = owner.shape[0]
    lane = valence.shape[2] // (2 * NZ * NY * NX)
    z, y, xh = lax.axis_index("z"), lax.axis_index("y"), lax.axis_index("xh")
    gp = lax.axis_index("xl") * 2 + lax.axis_index("c")
    me = jnp.stack([z, y, gp]).astype(jnp.int32)

    recv = lax.all_to_all(pack(valence), ("z", "y", "xh"), 0, 0, tiled=True)
    mine = jnp.concatenate([lax.dynamic_index_in_dim(recv, owner[b], 0, keepdims=False) for b in range(nb)], axis=0)

    other = shift(mine, "xh", NX, 1)
    lo, hi = jnp.where(xh == 0, mine, other), jnp.where(xh == 0, other, mine)
    a = jnp.concatenate([lo[:, :lane], hi[:, :lane]], axis=1)
    b = jnp.concatenate([lo[:, lane:], hi[:, lane:]], axis=1)

    ya = [a, shift(a, "y", NY, 1), shift(a, "y", NY, -1), shift(a, "y", NY, 2)]
    dys = [0, -1, 1, -2]
    zr = zl = b
    zb, dzs = [b], [0]
    hb = b.shape[0] // 2
    for s in (1, 2, 3):
        zr, zl = shift(zr, "z", NZ, 1), shift(zl, "z", NZ, -1)
        zb += [zr, zl]
        dzs += [-s, s]
    zb.append(jnp.concatenate([shift(zr[:hb], "z", NZ, 1), shift(zl[hb:], "z", NZ, -1)], axis=0))
    dzs.append(4)
    sa = jnp.stack(ya)
    sb = jnp.stack(zb)

    def at_a(dz):
        return [(0, dz, d) for d in dys]

    def at_b(dy):
        return [(1, d, dy) for d in dzs]

    a1r, a1l = shift(sa, "z", NZ, 1), shift(sa, "z", NZ, -1)
    a2r, a2l = shift(a1r, "z", NZ, 1), shift(a1l, "z", NZ, -1)
    acc = pair_call(me, screened, [sa, a1r, a1l], [at_a(0), at_a(-1), at_a(1)])
    a2r, a2l, acc = lax.optimization_barrier((a2r, a2l, acc))
    br, bl = shift(sb, "y", NY, 1), shift(sb, "y", NY, -1)
    a3r, a3l = shift(a2r, "z", NZ, 1), shift(a2l, "z", NZ, -1)
    acc = pair_call(me, screened, [sb, a2r, a2l], [at_b(0), at_a(-2), at_a(2)], acc)
    a3r, a3l, acc = lax.optimization_barrier((a3r, a3l, acc))
    a4r, a4l = shift(a3r[:2], "z", NZ, 1), shift(a3l[2:], "z", NZ, -1)
    b2r, b2l = shift(br[:4], "y", NY, 1), shift(bl[4:], "y", NY, -1)
    acc = pair_call(me, screened, [a3r, a3l, br, bl], [at_a(-3), at_a(3), at_b(-1), at_b(1)], acc)
    parts = pair_call(me, screened, [a4r, a4l, b2r, b2l], [at_a(4)[:2], at_a(4)[2:], at_b(2)[:4], at_b(2)[4:]], acc, last=True)

    sums = [parts[0]] + [lax.ppermute(parts[k], ("xl", "c"), [(i, i ^ k) for i in range(NGP)]) for k in (1, 2, 3)]
    term = term_call(sums, conduction)

    zsum = jnp.sum(lax.all_to_all(term, "z", 0, 0, tiled=True), axis=0)
    rows = zsum.T.reshape(NY * NX, zsum.shape[1] // (NY * NX), zsum.shape[0])
    return jnp.sum(lax.all_to_all(rows, ("y", "xh"), 0, 0, tiled=True), axis=0)


def solution(mesh):
    fine = Mesh(mesh.devices.reshape(NZ, NY, NX, 2, 2), ("z", "y", "xh", "xl", "c"))
    ga, gp = ("z", "y", "xh"), ("xl", "c")
    placed = (P(ga, gp), P(ga, None, gp), P(None, ga), P())
    return jax.shard_map(body, mesh=fine, in_specs=placed, out_specs=P(ga, gp), check_vma=False)
```

```python
import functools

import jax
import jax.numpy as jnp
from jax import lax
from jax.experimental import pallas as pl
from jax.experimental.pallas import tpu as pltpu
from jax.sharding import Mesh, PartitionSpec as P

NZ, NY, NX, NGP = 8, 4, 2, 4
K = 256
F32, BF16 = jnp.float32, jnp.bfloat16
VM = pl.BlockSpec(memory_space=pltpu.VMEM)
SM = pl.BlockSpec(memory_space=pltpu.SMEM)


def shift(x, axis, n, d):
    return lax.ppermute(x, axis, [(i, (i + d) % n) for i in range(n)])


def pack_kernel(lane, own_ref, out_ref):
    half = NZ * NY * NX * lane
    for z in range(NZ):
        for y in range(NY):
            for x in range(NX):
                p = (z * NY + y) * NX + x
                q = (y * NZ + z) * NX + x
                out_ref[p, :, :lane] = own_ref[0, :, p * lane:(p + 1) * lane]
                out_ref[p, :, lane:] = own_ref[0, :, half + q * lane:half + (q + 1) * lane]


def pack(valence):
    _, nv, ncol = valence.shape
    n = NZ * NY * NX
    lane = ncol // (2 * n)
    return pl.pallas_call(
        functools.partial(pack_kernel, lane),
        out_shape=jax.ShapeDtypeStruct((n, nv, 2 * lane), valence.dtype),
        in_specs=[VM],
        out_specs=VM,
        compiler_params=pltpu.CompilerParams(vmem_limit_bytes=8 << 20),
        cost_estimate=pl.CostEstimate(flops=0, bytes_accessed=4 * nv * ncol, transcendentals=0),
    )(valence)


def pair_kernel(places, first, last, me_ref, w_ref, *refs):
    blocks, rest = refs[:len(places)], refs[len(places):]
    z, y = me_ref[0], me_ref[1]
    half = w_ref.shape[1] // 2
    acc = None if first else rest[0][...]
    for ref, place in zip(blocks, places, strict=True):
        for i, (part, dz, dy) in enumerate(place):
            zz, yy = (z + dz) & (NZ - 1), (y + dy) & (NY - 1)
            column = (zz * NY + yy) * K if part == 0 else half + (yy * NZ + zz) * K
            w = w_ref[:, pl.ds(pl.multiple_of(column, K), K)]
            term = lax.dot_general(ref[i], w, (((1,), (1,)), ((), ())), preferred_element_type=F32)
            acc = term if acc is None else acc + term
    outs = rest[0 if first else 1:]
    if not last:
        outs[0][...] = acc
        return
    scratch = outs[NGP]
    scratch[...] = acc
    rows = outs[0].shape[0]
    for k in range(NGP):
        outs[k][...] = scratch[pl.ds(pl.multiple_of((me_ref[2] ^ k) * rows, 8), rows), :]


def pair_call(me, w, blocks, places, acc=None, last=False):
    n = sum(b.shape[0] for b in blocks)
    rows, g = blocks[0].shape[1], w.shape[0]
    args = [me, w, *blocks] + ([] if acc is None else [acc])
    whole = jax.ShapeDtypeStruct((rows, g), F32)
    share = jax.ShapeDtypeStruct((rows // NGP, g), F32)
    return pl.pallas_call(
        functools.partial(pair_kernel, places, acc is None, last),
        out_shape=[share] * NGP if last else whole,
        in_specs=[SM] + [VM] * (len(args) - 1),
        out_specs=[VM] * NGP if last else VM,
        scratch_shapes=[pltpu.VMEM((rows, g), F32)] if last else [],
        compiler_params=pltpu.CompilerParams(vmem_limit_bytes=16 << 20),
        cost_estimate=pl.CostEstimate(flops=2 * n * rows * g * K, bytes_accessed=n * (rows + g) * K * 2, transcendentals=0),
    )(*args)


def regroup(tile, group):
    n = tile.shape[0]
    row = lax.broadcasted_iota(jnp.int32, tile.shape, 0)
    column = lax.broadcasted_iota(jnp.int32, tile.shape, 1) // group
    s = 1
    while s < n:
        r, q = (row & s) != 0, (column & s) != 0
        lower = pltpu.roll(pltpu.roll(tile, n - s, 0), s * group, 1)
        upper = pltpu.roll(pltpu.roll(tile, s, 0), tile.shape[1] - s * group, 1)
        tile = jnp.where(r == q, tile, jnp.where(q, lower, upper))
        s *= 2
    return tile


def term_kernel(a_ref, b_ref, c_ref, d_ref, cond_ref, out_ref):
    total = (a_ref[...] + b_ref[...]) + (c_ref[...] + d_ref[...])
    rows = total.shape[0]
    hi = total.astype(BF16)
    rest = total - hi.astype(F32)
    mid = rest.astype(BF16)
    low = (rest - mid.astype(F32)).astype(BF16)
    stacked = jnp.concatenate([hi, mid, low], axis=0)
    prod = lax.dot_general(stacked, cond_ref[...], (((1,), (1,)), ((), ())), preferred_element_type=F32)
    term = prod[:rows] + (prod[rows:2 * rows] + prod[2 * rows:])
    for a in range(rows // 8):
        for t in range(term.shape[1] // 128):
            out_ref[8 * t:8 * t + 8, a, :] = regroup(term[8 * a:8 * a + 8, 128 * t:128 * t + 128], 16)
    out_ref[:, rows // 8:, :] = jnp.zeros((out_ref.shape[0], out_ref.shape[1] - rows // 8, 128), F32)


def term_call(parts, cond):
    rows, nc = parts[0].shape[0], cond.shape[0]
    return pl.pallas_call(
        term_kernel,
        out_shape=jax.ShapeDtypeStruct((NZ * NY * NX, 8, 128), F32),
        in_specs=[VM] * 5,
        out_specs=VM,
        compiler_params=pltpu.CompilerParams(vmem_limit_bytes=8 << 20),
        cost_estimate=pl.CostEstimate(flops=6 * rows * nc * cond.shape[1], bytes_accessed=nc * cond.shape[1] * 2, transcendentals=0),
    )(*parts, cond)


def final_kernel(x_ref, out_ref, scratch):
    total = jnp.sum(x_ref[...], axis=0)
    rows, columns = out_ref.shape
    scratch[...] = jnp.zeros(scratch.shape, F32)
    for b in range(8):
        moved = total if b == 0 else pltpu.roll(total, 128 - rows * b, 1)
        for a in range(columns // 8):
            scratch[8 * a + b:8 * a + b + 1, :] = moved[a:a + 1, :]
    out_ref[...] = scratch[...].T[:rows, :columns]


def final_call(x, shape):
    return pl.pallas_call(
        final_kernel,
        out_shape=jax.ShapeDtypeStruct(shape, F32),
        in_specs=[VM],
        out_specs=VM,
        scratch_shapes=[pltpu.VMEM((128, 128), F32)],
        compiler_params=pltpu.CompilerParams(vmem_limit_bytes=8 << 20),
        cost_estimate=pl.CostEstimate(flops=x.size, bytes_accessed=x.size * 4, transcendentals=0),
    )(x)


def body(screened, valence, conduction, owner):
    nb = owner.shape[0]
    lane = valence.shape[2] // (2 * NZ * NY * NX)
    z, y, xh = lax.axis_index("z"), lax.axis_index("y"), lax.axis_index("xh")
    gp = lax.axis_index("xl") * 2 + lax.axis_index("c")
    me = jnp.stack([z, y, gp]).astype(jnp.int32)

    recv = lax.all_to_all(pack(valence), ("z", "y", "xh"), 0, 0, tiled=True)
    mine = jnp.concatenate([lax.dynamic_index_in_dim(recv, owner[b], 0, keepdims=False) for b in range(nb)], axis=0)

    other = shift(mine, "xh", NX, 1)
    lo, hi = jnp.where(xh == 0, mine, other), jnp.where(xh == 0, other, mine)
    a = jnp.concatenate([lo[:, :lane], hi[:, :lane]], axis=1)
    b = jnp.concatenate([lo[:, lane:], hi[:, lane:]], axis=1)

    ya = [a, shift(a, "y", NY, 1), shift(a, "y", NY, -1), shift(a, "y", NY, 2)]
    dys = [0, -1, 1, -2]
    zr = zl = b
    zb, dzs = [b], [0]
    hb = b.shape[0] // 2
    for s in (1, 2, 3):
        zr, zl = shift(zr, "z", NZ, 1), shift(zl, "z", NZ, -1)
        zb += [zr, zl]
        dzs += [-s, s]
    zb.append(jnp.concatenate([shift(zr[:hb], "z", NZ, 1), shift(zl[hb:], "z", NZ, -1)], axis=0))
    dzs.append(4)
    sa = jnp.stack(ya)
    sb = jnp.stack(zb)

    def at_a(dz):
        return [(0, dz, d) for d in dys]

    def at_b(dy):
        return [(1, d, dy) for d in dzs]

    a1r, a1l = shift(sa, "z", NZ, 1), shift(sa, "z", NZ, -1)
    a2r, a2l = shift(a1r, "z", NZ, 1), shift(a1l, "z", NZ, -1)
    acc = pair_call(me, screened, [sa, a1r, a1l], [at_a(0), at_a(-1), at_a(1)])
    a2r, a2l, acc = lax.optimization_barrier((a2r, a2l, acc))
    br, bl = shift(sb, "y", NY, 1), shift(sb, "y", NY, -1)
    a3r, a3l = shift(a2r, "z", NZ, 1), shift(a2l, "z", NZ, -1)
    acc = pair_call(me, screened, [sb, a2r, a2l], [at_b(0), at_a(-2), at_a(2)], acc)
    a3r, a3l, acc = lax.optimization_barrier((a3r, a3l, acc))
    a4r, a4l = shift(a3r[:2], "z", NZ, 1), shift(a3l[2:], "z", NZ, -1)
    b2r, b2l = shift(br[:4], "y", NY, 1), shift(bl[4:], "y", NY, -1)
    acc = pair_call(me, screened, [a3r, a3l, br, bl], [at_a(-3), at_a(3), at_b(-1), at_b(1)], acc)
    parts = pair_call(me, screened, [a4r, a4l, b2r, b2l], [at_a(4)[:2], at_a(4)[2:], at_b(2)[:4], at_b(2)[4:]], acc, last=True)

    sums = [parts[0]] + [lax.ppermute(parts[k], ("xl", "c"), [(i, i ^ k) for i in range(NGP)]) for k in (1, 2, 3)]
    term = term_call(sums, conduction)

    recv = lax.all_to_all(term, ("z", "y", "xh"), 0, 0, tiled=True)
    return final_call(recv, (conduction.shape[0] // (NZ * NY * NX), nb * valence.shape[1] // NGP))


def solution(mesh):
    fine = Mesh(mesh.devices.reshape(NZ, NY, NX, 2, 2), ("z", "y", "xh", "xl", "c"))
    ga, gp = ("z", "y", "xh"), ("xl", "c")
    placed = (P(ga, gp), P(ga, None, gp), P(None, ga), P())
    return jax.shard_map(body, mesh=fine, in_specs=placed, out_specs=P(ga, gp), check_vma=False)
```

```python
import functools

import jax
import jax.numpy as jnp
from jax import lax
from jax.experimental import pallas as pl
from jax.experimental.pallas import tpu as pltpu
from jax.sharding import Mesh, PartitionSpec as P

NZ, NY, NX, NGP = 8, 4, 2, 4
K = 256
F32, BF16 = jnp.float32, jnp.bfloat16
VM = pl.BlockSpec(memory_space=pltpu.VMEM)
SM = pl.BlockSpec(memory_space=pltpu.SMEM)


def shift(x, axis, n, d):
    return lax.ppermute(x, axis, [(i, (i + d) % n) for i in range(n)])


def pack_kernel(own_ref, out_ref):
    half = NZ * NY * K
    for z in range(NZ):
        for y in range(NY):
            p, q = z * NY + y, y * NZ + z
            out_ref[p, :, :K] = own_ref[0, :, p * K:(p + 1) * K]
            out_ref[p, :, K:] = own_ref[0, :, half + q * K:half + (q + 1) * K]


def pack(valence):
    _, nv, ncol = valence.shape
    return pl.pallas_call(
        pack_kernel,
        out_shape=jax.ShapeDtypeStruct((NZ * NY, nv, 2 * K), valence.dtype),
        in_specs=[VM],
        out_specs=VM,
        compiler_params=pltpu.CompilerParams(vmem_limit_bytes=8 << 20),
        cost_estimate=pl.CostEstimate(flops=0, bytes_accessed=4 * nv * ncol, transcendentals=0),
    )(valence)


def pair_kernel(places, first, last, me_ref, w_ref, *refs):
    blocks, rest = refs[:len(places)], refs[len(places):]
    z, y = me_ref[0], me_ref[1]
    half = w_ref.shape[1] // 2
    acc = None if first else rest[0][...]
    for ref, place in zip(blocks, places, strict=True):
        for i, (part, dz, dy) in enumerate(place):
            zz, yy = (z + dz) & (NZ - 1), (y + dy) & (NY - 1)
            column = (zz * NY + yy) * K if part == 0 else half + (yy * NZ + zz) * K
            w = w_ref[:, pl.ds(pl.multiple_of(column, K), K)]
            term = lax.dot_general(ref[i], w, (((1,), (1,)), ((), ())), preferred_element_type=F32)
            acc = term if acc is None else acc + term
    outs = rest[0 if first else 1:]
    if not last:
        outs[0][...] = acc
        return
    scratch = outs[NGP]
    scratch[...] = acc
    rows = outs[0].shape[0]
    for k in range(NGP):
        outs[k][...] = scratch[pl.ds(pl.multiple_of((me_ref[2] ^ k) * rows, 8), rows), :]


def pair_call(me, w, blocks, places, acc=None, last=False):
    n = sum(b.shape[0] for b in blocks)
    rows, g = blocks[0].shape[1], w.shape[0]
    args = [me, w, *blocks] + ([] if acc is None else [acc])
    whole = jax.ShapeDtypeStruct((rows, g), F32)
    share = jax.ShapeDtypeStruct((rows // NGP, g), F32)
    return pl.pallas_call(
        functools.partial(pair_kernel, places, acc is None, last),
        out_shape=[share] * NGP if last else whole,
        in_specs=[SM] + [VM] * (len(args) - 1),
        out_specs=[VM] * NGP if last else VM,
        scratch_shapes=[pltpu.VMEM((rows, g), F32)] if last else [],
        compiler_params=pltpu.CompilerParams(vmem_limit_bytes=16 << 20),
        cost_estimate=pl.CostEstimate(flops=2 * n * rows * g * K, bytes_accessed=n * (rows + g) * K * 2, transcendentals=0),
    )(*args)


def regroup(tile, group):
    n = tile.shape[0]
    row = lax.broadcasted_iota(jnp.int32, tile.shape, 0)
    column = lax.broadcasted_iota(jnp.int32, tile.shape, 1) // group
    s = 1
    while s < n:
        r, q = (row & s) != 0, (column & s) != 0
        lower = pltpu.roll(pltpu.roll(tile, n - s, 0), s * group, 1)
        upper = pltpu.roll(pltpu.roll(tile, s, 0), tile.shape[1] - s * group, 1)
        tile = jnp.where(r == q, tile, jnp.where(q, lower, upper))
        s *= 2
    return tile


def term_kernel(a_ref, b_ref, c_ref, d_ref, cond_ref, out_ref):
    total = (a_ref[...] + b_ref[...]) + (c_ref[...] + d_ref[...])
    rows = total.shape[0]
    hi = total.astype(BF16)
    rest = total - hi.astype(F32)
    mid = rest.astype(BF16)
    low = (rest - mid.astype(F32)).astype(BF16)
    stacked = jnp.concatenate([hi, mid, low], axis=0)
    prod = lax.dot_general(stacked, cond_ref[...], (((1,), (1,)), ((), ())), preferred_element_type=F32)
    term = prod[:rows] + (prod[rows:2 * rows] + prod[2 * rows:])
    for a in range(rows // 8):
        for t in range(term.shape[1] // 128):
            out_ref[8 * t:8 * t + 8, a, :] = regroup(term[8 * a:8 * a + 8, 128 * t:128 * t + 128], 16)
    out_ref[:, rows // 8:, :] = jnp.zeros((out_ref.shape[0], out_ref.shape[1] - rows // 8, 128), F32)


def term_call(parts, cond):
    rows, nc = parts[0].shape[0], cond.shape[0]
    return pl.pallas_call(
        term_kernel,
        out_shape=jax.ShapeDtypeStruct((NZ * NY * NX, 8, 128), F32),
        in_specs=[VM] * 5,
        out_specs=VM,
        compiler_params=pltpu.CompilerParams(vmem_limit_bytes=8 << 20),
        cost_estimate=pl.CostEstimate(flops=6 * rows * nc * cond.shape[1], bytes_accessed=nc * cond.shape[1] * 2, transcendentals=0),
    )(*parts, cond)


def final_kernel(x_ref, out_ref, scratch):
    total = jnp.sum(x_ref[...], axis=0)
    rows, columns = out_ref.shape
    scratch[...] = jnp.zeros(scratch.shape, F32)
    for b in range(8):
        moved = total if b == 0 else pltpu.roll(total, 128 - rows * b, 1)
        for a in range(columns // 8):
            scratch[8 * a + b:8 * a + b + 1, :] = moved[a:a + 1, :]
    out_ref[...] = scratch[...].T[:rows, :columns]


def final_call(x, shape):
    return pl.pallas_call(
        final_kernel,
        out_shape=jax.ShapeDtypeStruct(shape, F32),
        in_specs=[VM],
        out_specs=VM,
        scratch_shapes=[pltpu.VMEM((128, 128), F32)],
        compiler_params=pltpu.CompilerParams(vmem_limit_bytes=8 << 20),
        cost_estimate=pl.CostEstimate(flops=x.size, bytes_accessed=x.size * 4, transcendentals=0),
    )(x)


def body(screened, valence, conduction, owner):
    nb = owner.shape[0]
    z, y, xh = lax.axis_index("z"), lax.axis_index("y"), lax.axis_index("xh")
    gp = lax.axis_index("xl") * 2 + lax.axis_index("c")
    me = jnp.stack([z, y, gp]).astype(jnp.int32)

    recv = lax.all_to_all(pack(valence), ("z", "y"), 0, 0, tiled=True)
    mine = jnp.stack([lax.dynamic_index_in_dim(recv, owner[b] // NX, 0, keepdims=False) for b in range(nb)])
    other = shift(mine, "xh", NX, 1)
    here = (owner % NX == xh)[:, None, None]
    a = jnp.where(here, mine[:, :, :K], other[:, :, :K]).reshape(-1, K)
    b = jnp.where(here, mine[:, :, K:], other[:, :, K:]).reshape(-1, K)

    ya = [a, shift(a, "y", NY, 1), shift(a, "y", NY, -1), shift(a, "y", NY, 2)]
    dys = [0, -1, 1, -2]
    dzs = [0, -1, 1, -2, 2, -3, 3, -4]
    z1r, z1l = shift(b, "z", NZ, 1), shift(b, "z", NZ, -1)
    sa, z1r, z1l = lax.optimization_barrier((jnp.stack(ya), z1r, z1l))
    a1r, a1l = shift(sa, "z", NZ, 1), shift(sa, "z", NZ, -1)
    z2r, z2l = shift(z1r, "z", NZ, 1), shift(z1l, "z", NZ, -1)
    acc = pair_call(me, screened, [sa], [[(0, 0, d) for d in dys]])
    a1r, a1l, z2r, z2l, acc = lax.optimization_barrier((a1r, a1l, z2r, z2l, acc))
    z3r, z3l = shift(z2r, "z", NZ, 1), shift(z2l, "z", NZ, -1)
    acc = pair_call(me, screened, [a1r, a1l], [[(0, -1, d) for d in dys], [(0, 1, d) for d in dys]], acc)
    z3r, z3l, acc = lax.optimization_barrier((z3r, z3l, acc))
    zb = [b, z1r, z1l, z2r, z2l, z3r, z3l, shift(z3r, "z", NZ, 1)]
    sb0, sb1 = jnp.stack(zb[:4]), jnp.stack(zb[4:])

    def at_a(dz):
        return [(0, dz, d) for d in dys]

    def at_b(dy, h):
        return [(1, d, dy) for d in dzs[4 * h:4 * h + 4]]

    a2r, a2l = shift(a1r, "z", NZ, 1), shift(a1l, "z", NZ, -1)
    br0, br1 = shift(sb0, "y", NY, 1), shift(sb1, "y", NY, 1)
    bl0, bl1 = shift(sb0, "y", NY, -1), shift(sb1, "y", NY, -1)
    a3r, a3l = shift(a2r, "z", NZ, 1), shift(a2l, "z", NZ, -1)
    acc = pair_call(me, screened, [sb0, sb1, a2r, a2l], [at_b(0, 0), at_b(0, 1), at_a(-2), at_a(2)], acc)
    a3r, a3l, acc = lax.optimization_barrier((a3r, a3l, acc))
    a4r, a4l = shift(a3r[:2], "z", NZ, 1), shift(a3l[2:], "z", NZ, -1)
    b2r, b2l = shift(br0, "y", NY, 1), shift(bl1, "y", NY, -1)
    acc = pair_call(me, screened, [a3r, a3l, br0, br1, bl0, bl1], [at_a(-3), at_a(3), at_b(-1, 0), at_b(-1, 1), at_b(1, 0), at_b(1, 1)], acc)
    parts = pair_call(me, screened, [a4r, a4l, b2r, b2l], [at_a(4)[:2], at_a(4)[2:], at_b(2, 0), at_b(2, 1)], acc, last=True)

    sums = [parts[0]] + [lax.ppermute(parts[k], ("xl", "c"), [(i, i ^ k) for i in range(NGP)]) for k in (1, 2, 3)]
    term = term_call(sums, conduction)

    recv = lax.all_to_all(term, ("z", "y", "xh"), 0, 0, tiled=True)
    return final_call(recv, (conduction.shape[0] // (NZ * NY * NX), nb * valence.shape[1] // NGP))


def solution(mesh):
    fine = Mesh(mesh.devices.reshape(NZ, NY, NX, 2, 2), ("z", "y", "xh", "xl", "c"))
    ga, gp = ("z", "y", "xh"), ("xl", "c")
    placed = (P(ga, gp), P(ga, None, gp), P(None, ga), P())
    return jax.shard_map(body, mesh=fine, in_specs=placed, out_specs=P(ga, gp), check_vma=False)
```

```python
import functools

import jax
import jax.numpy as jnp
from jax import lax
from jax.experimental import pallas as pl
from jax.experimental.pallas import tpu as pltpu
from jax.sharding import Mesh, PartitionSpec as P

NZ, NY, NX, NGP = 8, 4, 2, 4
K = 256
F32, BF16 = jnp.float32, jnp.bfloat16
VM = pl.BlockSpec(memory_space=pltpu.VMEM)
SM = pl.BlockSpec(memory_space=pltpu.SMEM)


def shift(x, axis, n, d):
    return lax.ppermute(x, axis, [(i, (i + d) % n) for i in range(n)])


def pack_kernel(own_ref, out_ref):
    half = NZ * NY * K
    for z in range(NZ):
        for y in range(NY):
            p, q = z * NY + y, y * NZ + z
            out_ref[p, :, :K] = own_ref[0, :, p * K:(p + 1) * K]
            out_ref[p, :, K:] = own_ref[0, :, half + q * K:half + (q + 1) * K]


def pack(valence):
    _, nv, ncol = valence.shape
    return pl.pallas_call(
        pack_kernel,
        out_shape=jax.ShapeDtypeStruct((NZ * NY, nv, 2 * K), valence.dtype),
        in_specs=[VM],
        out_specs=VM,
        compiler_params=pltpu.CompilerParams(vmem_limit_bytes=8 << 20),
        cost_estimate=pl.CostEstimate(flops=0, bytes_accessed=4 * nv * ncol, transcendentals=0),
    )(valence)


def pair_kernel(places, first, last, me_ref, w_ref, *refs):
    blocks, rest = refs[:len(places)], refs[len(places):]
    z, y = me_ref[0], me_ref[1]
    half = w_ref.shape[1] // 2
    acc = None if first else rest[0][...]
    for ref, place in zip(blocks, places, strict=True):
        for i, (part, dz, dy) in enumerate(place):
            zz, yy = (z + dz) & (NZ - 1), (y + dy) & (NY - 1)
            column = (zz * NY + yy) * K if part == 0 else half + (yy * NZ + zz) * K
            w = w_ref[:, pl.ds(pl.multiple_of(column, K), K)]
            term = lax.dot_general(ref[i], w, (((1,), (1,)), ((), ())), preferred_element_type=F32)
            acc = term if acc is None else acc + term
    outs = rest[0 if first else 1:]
    if not last:
        outs[0][...] = acc
        return
    scratch = outs[NGP]
    scratch[...] = acc
    rows = outs[0].shape[0]
    for k in range(NGP):
        outs[k][...] = scratch[pl.ds(pl.multiple_of((me_ref[2] ^ k) * rows, 8), rows), :]


def pair_call(me, w, blocks, places, acc=None, last=False):
    n = sum(b.shape[0] for b in blocks)
    rows, g = blocks[0].shape[1], w.shape[0]
    args = [me, w, *blocks] + ([] if acc is None else [acc])
    whole = jax.ShapeDtypeStruct((rows, g), F32)
    share = jax.ShapeDtypeStruct((rows // NGP, g), F32)
    return pl.pallas_call(
        functools.partial(pair_kernel, places, acc is None, last),
        out_shape=[share] * NGP if last else whole,
        in_specs=[SM] + [VM] * (len(args) - 1),
        out_specs=[VM] * NGP if last else VM,
        scratch_shapes=[pltpu.VMEM((rows, g), F32)] if last else [],
        compiler_params=pltpu.CompilerParams(vmem_limit_bytes=16 << 20),
        cost_estimate=pl.CostEstimate(flops=2 * n * rows * g * K, bytes_accessed=n * (rows + g) * K * 2, transcendentals=0),
    )(*args)


def regroup(tile, group):
    n = tile.shape[0]
    row = lax.broadcasted_iota(jnp.int32, tile.shape, 0)
    column = lax.broadcasted_iota(jnp.int32, tile.shape, 1) // group
    s = 1
    while s < n:
        r, q = (row & s) != 0, (column & s) != 0
        lower = pltpu.roll(pltpu.roll(tile, n - s, 0), s * group, 1)
        upper = pltpu.roll(pltpu.roll(tile, s, 0), tile.shape[1] - s * group, 1)
        tile = jnp.where(r == q, tile, jnp.where(q, lower, upper))
        s *= 2
    return tile


def term_kernel(a_ref, b_ref, c_ref, d_ref, cond_ref, out_ref):
    total = (a_ref[...] + b_ref[...]) + (c_ref[...] + d_ref[...])
    rows = total.shape[0]
    hi = total.astype(BF16)
    rest = total - hi.astype(F32)
    mid = rest.astype(BF16)
    low = (rest - mid.astype(F32)).astype(BF16)
    stacked = jnp.concatenate([hi, mid, low], axis=0)
    prod = lax.dot_general(stacked, cond_ref[...], (((1,), (1,)), ((), ())), preferred_element_type=F32)
    term = prod[:rows] + (prod[rows:2 * rows] + prod[2 * rows:])
    for a in range(rows // 8):
        for t in range(term.shape[1] // 128):
            out_ref[8 * t:8 * t + 8, a, :] = regroup(term[8 * a:8 * a + 8, 128 * t:128 * t + 128], 16)
    out_ref[:, rows // 8:, :] = jnp.zeros((out_ref.shape[0], out_ref.shape[1] - rows // 8, 128), F32)


def term_call(parts, cond):
    rows, nc = parts[0].shape[0], cond.shape[0]
    return pl.pallas_call(
        term_kernel,
        out_shape=jax.ShapeDtypeStruct((NZ * NY * NX, 8, 128), F32),
        in_specs=[VM] * 5,
        out_specs=VM,
        compiler_params=pltpu.CompilerParams(vmem_limit_bytes=8 << 20),
        cost_estimate=pl.CostEstimate(flops=6 * rows * nc * cond.shape[1], bytes_accessed=nc * cond.shape[1] * 2, transcendentals=0),
    )(*parts, cond)


def final_kernel(x_ref, out_ref, scratch):
    total = jnp.sum(x_ref[...], axis=0)
    rows, columns = out_ref.shape
    scratch[...] = jnp.zeros(scratch.shape, F32)
    for b in range(8):
        moved = total if b == 0 else pltpu.roll(total, 128 - rows * b, 1)
        for a in range(columns // 8):
            scratch[8 * a + b:8 * a + b + 1, :] = moved[a:a + 1, :]
    out_ref[...] = scratch[...].T[:rows, :columns]


def final_call(x, shape):
    return pl.pallas_call(
        final_kernel,
        out_shape=jax.ShapeDtypeStruct(shape, F32),
        in_specs=[VM],
        out_specs=VM,
        scratch_shapes=[pltpu.VMEM((128, 128), F32)],
        compiler_params=pltpu.CompilerParams(vmem_limit_bytes=8 << 20),
        cost_estimate=pl.CostEstimate(flops=x.size, bytes_accessed=x.size * 4, transcendentals=0),
    )(x)


def body(screened, valence, conduction, owner):
    nb = owner.shape[0]
    z, y, xh = lax.axis_index("z"), lax.axis_index("y"), lax.axis_index("xh")
    gp = lax.axis_index("xl") * 2 + lax.axis_index("c")
    me = jnp.stack([z, y, gp]).astype(jnp.int32)

    recv = lax.all_to_all(pack(valence), ("z", "y"), 0, 0, tiled=True)
    mine = jnp.stack([lax.dynamic_index_in_dim(recv, owner[b] // NX, 0, keepdims=False) for b in range(nb)])
    other = shift(mine, "xh", NX, 1)
    here = (owner % NX == xh)[:, None, None]
    a = jnp.where(here, mine[:, :, :K], other[:, :, :K]).reshape(-1, K)
    b = jnp.where(here, mine[:, :, K:], other[:, :, K:]).reshape(-1, K)

    ya = [a, shift(a, "y", NY, 1), shift(a, "y", NY, -1), shift(a, "y", NY, 2)]
    dys = [0, -1, 1, -2]
    dzs = [0, -1, 1, -2, 2, -3, 3, -4]
    z1r, z1l = shift(b, "z", NZ, 1), shift(b, "z", NZ, -1)
    sa, z1r, z1l = lax.optimization_barrier((jnp.stack(ya), z1r, z1l))
    a1r, a1l = shift(sa, "z", NZ, 1), shift(sa, "z", NZ, -1)
    z2r, z2l = shift(z1r, "z", NZ, 1), shift(z1l, "z", NZ, -1)
    acc = pair_call(me, screened, [sa], [[(0, 0, d) for d in dys]])
    a1r, a1l, z2r, z2l, acc = lax.optimization_barrier((a1r, a1l, z2r, z2l, acc))
    z3r, z3l = shift(z2r, "z", NZ, 1), shift(z2l, "z", NZ, -1)
    z4 = shift(z2l, "z", NZ, -2)
    acc = pair_call(me, screened, [a1r, a1l], [[(0, -1, d) for d in dys], [(0, 1, d) for d in dys]], acc)
    z3r, z3l, z4, acc = lax.optimization_barrier((z3r, z3l, z4, acc))
    zb = [b, z1r, z1l, z2r, z2l, z3r, z3l, z4]
    sb0, sb1 = jnp.stack(zb[:4]), jnp.stack(zb[4:])

    def at_a(dz):
        return [(0, dz, d) for d in dys]

    def at_b(dy, h):
        return [(1, d, dy) for d in dzs[4 * h:4 * h + 4]]

    a2r, a2l = shift(a1r, "z", NZ, 1), shift(a1l, "z", NZ, -1)
    br0, bl0 = shift(sb0, "y", NY, 1), shift(sb0, "y", NY, -1)
    sb1, br0, bl0 = lax.optimization_barrier((sb1, br0, bl0))
    br1, bl1 = shift(sb1, "y", NY, 1), shift(sb1, "y", NY, -1)
    a3r, a3l = shift(a2r, "z", NZ, 1), shift(a2l, "z", NZ, -1)
    acc = pair_call(me, screened, [sb0, sb1, a2r, a2l], [at_b(0, 0), at_b(0, 1), at_a(-2), at_a(2)], acc)
    a3r, a3l, acc = lax.optimization_barrier((a3r, a3l, acc))
    a4r, a4l = shift(a3r[:2], "z", NZ, 1), shift(a3l[2:], "z", NZ, -1)
    b2r, b2l = shift(br0, "y", NY, 1), shift(bl1, "y", NY, -1)
    acc = pair_call(me, screened, [a3r, a3l, br0, br1, bl0, bl1], [at_a(-3), at_a(3), at_b(-1, 0), at_b(-1, 1), at_b(1, 0), at_b(1, 1)], acc)
    parts = pair_call(me, screened, [a4r, a4l, b2r, b2l], [at_a(4)[:2], at_a(4)[2:], at_b(2, 0), at_b(2, 1)], acc, last=True)

    sums = [parts[0]] + [lax.ppermute(parts[k], ("xl", "c"), [(i, i ^ k) for i in range(NGP)]) for k in (1, 2, 3)]
    term = term_call(sums, conduction)

    recv = lax.all_to_all(term, ("z", "y", "xh"), 0, 0, tiled=True)
    return final_call(recv, (conduction.shape[0] // (NZ * NY * NX), nb * valence.shape[1] // NGP))


def solution(mesh):
    fine = Mesh(mesh.devices.reshape(NZ, NY, NX, 2, 2), ("z", "y", "xh", "xl", "c"))
    ga, gp = ("z", "y", "xh"), ("xl", "c")
    placed = (P(ga, gp), P(ga, None, gp), P(None, ga), P())
    return jax.shard_map(body, mesh=fine, in_specs=placed, out_specs=P(ga, gp), check_vma=False)
```

```python
import functools

import jax
import jax.numpy as jnp
from jax import lax
from jax.experimental import pallas as pl
from jax.experimental.pallas import tpu as pltpu
from jax.sharding import Mesh, PartitionSpec as P

NZ, NY, NX, NGP = 8, 4, 2, 4
K = 256
F32, BF16 = jnp.float32, jnp.bfloat16
VM = pl.BlockSpec(memory_space=pltpu.VMEM)
SM = pl.BlockSpec(memory_space=pltpu.SMEM)


def shift(x, axis, n, d):
    return lax.ppermute(x, axis, [(i, (i + d) % n) for i in range(n)])


def pack_kernel(own_ref, out_ref):
    half = NZ * NY * K
    for z in range(NZ):
        for y in range(NY):
            p, q = z * NY + y, y * NZ + z
            out_ref[p, :, :K] = own_ref[0, :, p * K:(p + 1) * K]
            out_ref[p, :, K:] = own_ref[0, :, half + q * K:half + (q + 1) * K]


def pack(valence):
    _, nv, ncol = valence.shape
    return pl.pallas_call(
        pack_kernel,
        out_shape=jax.ShapeDtypeStruct((NZ * NY, nv, 2 * K), valence.dtype),
        in_specs=[VM],
        out_specs=VM,
        compiler_params=pltpu.CompilerParams(vmem_limit_bytes=8 << 20),
        cost_estimate=pl.CostEstimate(flops=0, bytes_accessed=4 * nv * ncol, transcendentals=0),
    )(valence)


def pair_kernel(places, first, last, me_ref, w_ref, *refs):
    blocks, rest = refs[:len(places)], refs[len(places):]
    z, y = me_ref[0], me_ref[1]
    half = w_ref.shape[1] // 2
    acc = None if first else rest[0][...]
    for ref, place in zip(blocks, places, strict=True):
        for i, (part, dz, dy) in enumerate(place):
            zz, yy = (z + dz) & (NZ - 1), (y + dy) & (NY - 1)
            column = (zz * NY + yy) * K if part == 0 else half + (yy * NZ + zz) * K
            w = w_ref[:, pl.ds(pl.multiple_of(column, K), K)]
            term = lax.dot_general(ref[i], w, (((1,), (1,)), ((), ())), preferred_element_type=F32)
            acc = term if acc is None else acc + term
    outs = rest[0 if first else 1:]
    if not last:
        outs[0][...] = acc
        return
    scratch = outs[NGP]
    scratch[...] = acc
    rows = outs[0].shape[0]
    for k in range(NGP):
        outs[k][...] = scratch[pl.ds(pl.multiple_of((me_ref[2] ^ k) * rows, 8), rows), :]


def pair_call(me, w, blocks, places, acc=None, last=False):
    n = sum(b.shape[0] for b in blocks)
    rows, g = blocks[0].shape[1], w.shape[0]
    args = [me, w, *blocks] + ([] if acc is None else [acc])
    whole = jax.ShapeDtypeStruct((rows, g), F32)
    share = jax.ShapeDtypeStruct((rows // NGP, g), F32)
    return pl.pallas_call(
        functools.partial(pair_kernel, places, acc is None, last),
        out_shape=[share] * NGP if last else whole,
        in_specs=[SM] + [VM] * (len(args) - 1),
        out_specs=[VM] * NGP if last else VM,
        scratch_shapes=[pltpu.VMEM((rows, g), F32)] if last else [],
        compiler_params=pltpu.CompilerParams(vmem_limit_bytes=16 << 20),
        cost_estimate=pl.CostEstimate(flops=2 * n * rows * g * K, bytes_accessed=n * (rows + g) * K * 2, transcendentals=0),
    )(*args)


def regroup(tile, group):
    n = tile.shape[0]
    row = lax.broadcasted_iota(jnp.int32, tile.shape, 0)
    column = lax.broadcasted_iota(jnp.int32, tile.shape, 1) // group
    s = 1
    while s < n:
        r, q = (row & s) != 0, (column & s) != 0
        lower = pltpu.roll(pltpu.roll(tile, n - s, 0), s * group, 1)
        upper = pltpu.roll(pltpu.roll(tile, s, 0), tile.shape[1] - s * group, 1)
        tile = jnp.where(r == q, tile, jnp.where(q, lower, upper))
        s *= 2
    return tile


def term_kernel(a_ref, b_ref, c_ref, d_ref, cond_ref, out_ref):
    total = (a_ref[...] + b_ref[...]) + (c_ref[...] + d_ref[...])
    rows = total.shape[0]
    hi = total.astype(BF16)
    rest = total - hi.astype(F32)
    mid = rest.astype(BF16)
    low = (rest - mid.astype(F32)).astype(BF16)
    stacked = jnp.concatenate([hi, mid, low], axis=0)
    prod = lax.dot_general(stacked, cond_ref[...], (((1,), (1,)), ((), ())), preferred_element_type=F32)
    term = prod[:rows] + (prod[rows:2 * rows] + prod[2 * rows:])
    for a in range(rows // 8):
        for t in range(term.shape[1] // 128):
            out_ref[8 * t:8 * t + 8, a, :] = regroup(term[8 * a:8 * a + 8, 128 * t:128 * t + 128], 16)
    out_ref[:, rows // 8:, :] = jnp.zeros((out_ref.shape[0], out_ref.shape[1] - rows // 8, 128), F32)


def term_call(parts, cond):
    rows, nc = parts[0].shape[0], cond.shape[0]
    return pl.pallas_call(
        term_kernel,
        out_shape=jax.ShapeDtypeStruct((NZ * NY * NX, 8, 128), F32),
        in_specs=[VM] * 5,
        out_specs=VM,
        compiler_params=pltpu.CompilerParams(vmem_limit_bytes=8 << 20),
        cost_estimate=pl.CostEstimate(flops=6 * rows * nc * cond.shape[1], bytes_accessed=nc * cond.shape[1] * 2, transcendentals=0),
    )(*parts, cond)


def final_kernel(x_ref, out_ref, scratch):
    total = jnp.sum(x_ref[...], axis=0)
    rows, columns = out_ref.shape
    scratch[...] = jnp.zeros(scratch.shape, F32)
    for b in range(8):
        moved = total if b == 0 else pltpu.roll(total, 128 - rows * b, 1)
        for a in range(columns // 8):
            scratch[8 * a + b:8 * a + b + 1, :] = moved[a:a + 1, :]
    out_ref[...] = scratch[...].T[:rows, :columns]


def final_call(x, shape):
    return pl.pallas_call(
        final_kernel,
        out_shape=jax.ShapeDtypeStruct(shape, F32),
        in_specs=[VM],
        out_specs=VM,
        scratch_shapes=[pltpu.VMEM((128, 128), F32)],
        compiler_params=pltpu.CompilerParams(vmem_limit_bytes=8 << 20),
        cost_estimate=pl.CostEstimate(flops=x.size, bytes_accessed=x.size * 4, transcendentals=0),
    )(x)


def body(screened, valence, conduction, owner):
    nb = owner.shape[0]
    z, y, xh = lax.axis_index("z"), lax.axis_index("y"), lax.axis_index("xh")
    gp = lax.axis_index("xl") * 2 + lax.axis_index("c")
    me = jnp.stack([z, y, gp]).astype(jnp.int32)

    recv = lax.all_to_all(pack(valence), ("z", "y"), 0, 0, tiled=True)
    mine = jnp.stack([lax.dynamic_index_in_dim(recv, owner[b] // NX, 0, keepdims=False) for b in range(nb)])
    other = shift(mine, "xh", NX, 1)
    here = (owner % NX == xh)[:, None, None]
    a = jnp.where(here, mine[:, :, :K], other[:, :, :K]).reshape(-1, K)
    b = jnp.where(here, mine[:, :, K:], other[:, :, K:]).reshape(-1, K)

    ya = [a, shift(a, "y", NY, 1), shift(a, "y", NY, -1), shift(a, "y", NY, 2)]
    dys = [0, -1, 1, -2]
    dzs = [0, -1, 1, -2, 2, -3, 3, -4]
    z1r, z1l = shift(b, "z", NZ, 1), shift(b, "z", NZ, -1)
    sa, z1r, z1l = lax.optimization_barrier((jnp.stack(ya), z1r, z1l))
    a1r, a1l = shift(sa, "z", NZ, 1), shift(sa, "z", NZ, -1)
    z2r, z2l = shift(z1r, "z", NZ, 1), shift(z1l, "z", NZ, -1)
    acc = pair_call(me, screened, [sa], [[(0, 0, d) for d in dys]])
    a1r, a1l, z2r, z2l, acc = lax.optimization_barrier((a1r, a1l, z2r, z2l, acc))
    z3r, z3l = shift(z2r, "z", NZ, 1), shift(z2l, "z", NZ, -1)
    z4 = shift(z2l, "z", NZ, -2)
    zb = [b, z1r, z1l, z2r, z2l, z3r, z3l, z4]
    sb0, sb1 = jnp.stack(zb[:4]), jnp.stack(zb[4:])

    def at_a(dz):
        return [(0, dz, d) for d in dys]

    def at_b(dy, h):
        return [(1, d, dy) for d in dzs[4 * h:4 * h + 4]]

    a2r, a2l = shift(a1r, "z", NZ, 1), shift(a1l, "z", NZ, -1)
    br0, bl0 = shift(sb0, "y", NY, 1), shift(sb0, "y", NY, -1)
    sb1, br0, bl0 = lax.optimization_barrier((sb1, br0, bl0))
    br1, bl1 = shift(sb1, "y", NY, 1), shift(sb1, "y", NY, -1)
    a3r, a3l = shift(a2r, "z", NZ, 1), shift(a2l, "z", NZ, -1)
    acc = pair_call(me, screened, [a1r, a1l, sb0, sb1, a2r, a2l], [at_a(-1), at_a(1), at_b(0, 0), at_b(0, 1), at_a(-2), at_a(2)], acc)
    a3r, a3l, acc = lax.optimization_barrier((a3r, a3l, acc))
    a4r, a4l = shift(a3r[:2], "z", NZ, 1), shift(a3l[2:], "z", NZ, -1)
    b2r, b2l = shift(br0, "y", NY, 1), shift(bl1, "y", NY, -1)
    acc = pair_call(me, screened, [a3r, a3l, br0, br1, bl0, bl1], [at_a(-3), at_a(3), at_b(-1, 0), at_b(-1, 1), at_b(1, 0), at_b(1, 1)], acc)
    parts = pair_call(me, screened, [a4r, a4l, b2r, b2l], [at_a(4)[:2], at_a(4)[2:], at_b(2, 0), at_b(2, 1)], acc, last=True)

    sums = [parts[0]] + [lax.ppermute(parts[k], ("xl", "c"), [(i, i ^ k) for i in range(NGP)]) for k in (1, 2, 3)]
    term = term_call(sums, conduction)

    recv = lax.all_to_all(term, ("z", "y", "xh"), 0, 0, tiled=True)
    return final_call(recv, (conduction.shape[0] // (NZ * NY * NX), nb * valence.shape[1] // NGP))


def solution(mesh):
    fine = Mesh(mesh.devices.reshape(NZ, NY, NX, 2, 2), ("z", "y", "xh", "xl", "c"))
    ga, gp = ("z", "y", "xh"), ("xl", "c")
    placed = (P(ga, gp), P(ga, None, gp), P(None, ga), P())
    return jax.shard_map(body, mesh=fine, in_specs=placed, out_specs=P(ga, gp), check_vma=False)
```
